32 devices in a mesh: groups: 2 (over x), wide: 16 (over z, y, core).
Axes of the slice: x: 2, y: 2, z: 4, core: 2. Of those that a mesh axis runs over, the one named last changes fastest.
Arguments:
- iterate: float32 [8192, 128], P(('groups', 'wide')), parts along dimension 0, may hold values from -6 to 6
- rhs: float32 [8192, 128], P(('groups', 'wide')), parts along dimension 0, may hold values from -6 to 6
- schur: float32 [32, 384, 384], P(('groups', 'wide')), parts along dimension 0
- near_block: float32 [8192, 256], P(('groups', 'wide')), parts along dimension 0
- u_basis: float32 [32, 32, 4096], P('groups', None, 'wide'), parts along dimension 0, may hold values from -0.375 to 0.375
- v_basis: float32 [32, 32, 4096], P('groups', None, 'wide'), parts along dimension 0, may hold values from -0.375 to 0.375
- tile_rank: int32 [32, 16], P('groups', 'wide'), parts along dimension 0, may hold values from 1 to 32
- send_rows: int32 [32, 3, 128], P(('groups', 'wide')), parts along dimension 0, may hold values from 0 to 255
- send_count: int32 [32, 3], P(('groups', 'wide')), parts along dimension 0, may hold values from 0 to 128, as said below
- precond: float32 [8192], P(('groups', 'wide')), parts along dimension 0, may hold values from 0.1 to 1
Outputs:
- updated: float32 [8192, 128], P(('groups', 'wide')), parts along dimension 0
- residual: float32 [8192, 128], P(('groups', 'wide')), parts along dimension 0
The draws below stay inside these ranges and needn't reach their ends.
There are 2 independent parts, one for each index of `groups`. The reference program is written for one: setup_inputs(seed, part) draws one part's arguments, and reference() takes and returns one part's arrays. A program takes and returns all parts, laid end to end along the dimension named above; each array names one. Nothing has to cross between parts.
Inputs may be any that keep to these rules, and one draw needn't show every extreme that they name: send_count[p, 0] is 0 for p = 0 and send_count[p, 2] is 0 for p = 15; a block is full in every draw.
All inputs are finite; a program needn't handle non-finite values.
Results may differ from the reference program's by a relative error of at most 0.0003.
Values sent between devices are 32-bit elements; how exact they have to be, the bound alone decides.
A program may use at most 64 MiB of HBM per device.

```python
import math
import jax
import jax.numpy as jnp
from jax import lax

R_DEV = 256
LOADS = 128
K = 32
FB = 128
NS = 384
TILES = 16
N = 4096


def draw_schur(key, part):
    key_off = jax.random.fold_in(key, 11)
    key_diag = jax.random.fold_in(key, 12)
    off_diag = jax.random.normal(key_off, (TILES, NS, NS), jnp.float32)
    off_diag = off_diag * (0.5 / jnp.sqrt(jnp.float32(NS)))
    diag = jax.random.uniform(key_diag, (TILES, NS), jnp.float32, 1.5, 3.0)
    return off_diag + diag[:, :, None] * jnp.eye(NS, dtype=jnp.float32)[None]


def draw_near_block(key, part):
    key_off = jax.random.fold_in(key, 21)
    key_diag = jax.random.fold_in(key, 22)
    off_diag = jax.random.normal(key_off, (N, R_DEV), jnp.float32)
    off_diag = off_diag * (0.5 / jnp.sqrt(jnp.float32(R_DEV)))
    diag = jax.random.uniform(key_diag, (N, 1), jnp.float32, 0.5, 1.5)
    eye_rows = jnp.tile(jnp.eye(R_DEV, dtype=jnp.float32), (TILES, 1))
    return off_diag + diag * eye_rows


def draw_tile_rank(key, part):
    ranks = jax.random.randint(jax.random.fold_in(key, 31), (TILES, TILES), 1, K + 1, dtype=jnp.int32)
    return ranks.at[0, 1].set(1).at[1, 0].set(K)


def draw_send_count(key, part):
    counts = jax.random.randint(jax.random.fold_in(key, 41), (TILES, 3), 0, FB + 1, dtype=jnp.int32)
    owner = jnp.arange(TILES, dtype=jnp.int32)[:, None]
    offset = jnp.arange(3, dtype=jnp.int32)[None, :] - 1
    target = owner + offset
    inside = (target >= 0) & (target < TILES)
    counts = jnp.where(inside, counts, 0)
    return counts.at[1, 1].set(FB)


def touch_ends(drawn, stream_key, low, high):
    longest = drawn.shape.index(max(drawn.shape))
    spots = []
    for shift in (0, 1):
        where = [jax.random.randint(jax.random.fold_in(stream_key, axis), (), 0, length) for axis, length in enumerate(drawn.shape)]
        where[longest] = (where[longest] + shift) % drawn.shape[longest]
        spots.append(tuple(where))
    return drawn.at[spots[0]].set(low).at[spots[1]].set(high)


def raised(drawn, key, source, target, parts, factor):
    def block_of(axis_at):
        return (jnp.arange(drawn.shape[axis_at]) // (drawn.shape[axis_at] // parts)).reshape((-1,) + (1,) * (drawn.ndim - 1 - axis_at))

    one_side = jax.random.permutation(key, parts)[block_of(target)]
    second = (block_of(target) + parts // 2) % parts
    return jnp.where((block_of(source) == one_side) | (block_of(source) == second), factor * drawn, drawn)


def block_scale(rng, shape, shards, smallest, high):
    factor_of = 1.0
    for dim, blocks in shards:
        heights = jax.random.uniform(jax.random.fold_in(jax.random.fold_in(rng, 6), dim), (blocks,), jnp.float32, smallest / len(shards), high / len(shards))
        factor_of = factor_of * jnp.repeat(jnp.exp(heights), shape[dim] // blocks).reshape((-1,) + (1,) * (len(shape) - 1 - dim))
    return factor_of


def scatter_about(rng, shape, width, limit, split=(), kind=jnp.bfloat16):
    result = jax.random.normal(rng, shape, jnp.float32) * width
    if len(split) > 0:
        result = block_scale(rng, shape, split, -0.22, 0.18) * result
    return jnp.clip(result, min=-limit, max=limit).astype(kind)


def noise_with(stream_key, extent, spread, bound, split, heavy, held_as=jnp.bfloat16):
    entries = spread * jax.random.normal(stream_key, extent, jnp.float32)
    if split:
        entries = entries * block_scale(stream_key, extent, split, -0.22, 0.18)
    return jnp.clip(raised(entries, jax.random.fold_in(stream_key, 3), *heavy), -bound, bound).astype(held_as)


def setup_inputs(seed: int = 0, part: int = 0) -> dict:
    splits = jax.random.split(jax.random.key(seed), 11)
    part_splits = jax.random.split(jax.random.fold_in(splits[10], part), 11)
    iterate = scatter_about(part_splits[0], (N, LOADS), 1.0, 6.0, ((0, 16),), jnp.float32)
    rhs = scatter_about(part_splits[1], (N, LOADS), 1.0, 6.0, ((0, 16),), jnp.float32)
    schur = draw_schur(jax.random.fold_in(jax.random.fold_in(splits[10], part), 71), part)
    near_block = draw_near_block(jax.random.fold_in(jax.random.fold_in(splits[10], part), 71), part)
    u_basis = noise_with(part_splits[4], (TILES, K, N), (TILES * K) ** -0.5, 0.375, ((2, 16),), (0, 2, 16, 2.0), jnp.float32)
    v_basis = scatter_about(part_splits[5], (TILES, K, N), R_DEV ** -0.5, 0.375, ((2, 16),), jnp.float32)
    tile_rank = draw_tile_rank(jax.random.fold_in(jax.random.fold_in(splits[10], part), 71), part)
    send_rows = touch_ends(jax.random.randint(part_splits[7], (TILES, 3, FB), 0, R_DEV), jax.random.fold_in(part_splits[7], 1), 0, R_DEV - 1).astype(jnp.int32)
    send_count = draw_send_count(jax.random.fold_in(jax.random.fold_in(splits[10], part), 71), part)
    precond = jnp.clip(jnp.exp(math.log(1.0) - 2.3025851 * jax.random.uniform(part_splits[9], (N,), jnp.float32) ** block_scale(part_splits[9], (N,), ((0, 16),), -0.2, 0.2)), 0.1, 1.0)
    return {"iterate": iterate, "rhs": rhs, "schur": schur, "near_block": near_block, "u_basis": u_basis, "v_basis": v_basis, "tile_rank": tile_rank, "send_rows": send_rows, "send_count": send_count, "precond": precond}


def reference(iterate, rhs, schur, near_block, u_basis, v_basis, tile_rank, send_rows, send_count, precond):
    highest = lax.Precision.HIGHEST
    rows_local = jnp.arange(R_DEV, dtype=jnp.int32)
    slot_ids = jnp.arange(FB, dtype=jnp.int32)
    blocks = iterate.reshape(TILES, R_DEV, LOADS)
    valid = slot_ids[None, None, :] < send_count[:, :, None]
    select = ((send_rows[..., None] == rows_local) & valid[..., None]).astype(iterate.dtype)
    outgoing = jnp.einsum('posr,prl->posl', select, blocks, precision=highest)
    zero_block = jnp.zeros((1, 3, FB, LOADS), iterate.dtype)
    out_pad = jnp.concatenate([zero_block, outgoing, zero_block], axis=0)
    incoming = jnp.stack([out_pad[2:, 0], out_pad[1:-1, 1], out_pad[:-2, 2]], axis=1)
    forces = jnp.einsum('dab,dbl->dal', schur, incoming.reshape(TILES, NS, LOADS), precision=highest)
    forces = forces.reshape(TILES, 3, FB, LOADS)
    force_pad = jnp.concatenate([zero_block, forces, zero_block], axis=0)
    returned = jnp.stack([force_pad[:-2, 0], force_pad[1:-1, 1], force_pad[2:, 2]], axis=1)
    fem = jnp.einsum('posr,posl->prl', select, returned, precision=highest).reshape(N, LOADS)
    rank_ids = jnp.arange(K, dtype=jnp.int32)

    def tile_row(index):
        v_row = v_basis[index].reshape(K, TILES, R_DEV)
        coeff = jnp.einsum('kjr,jrl->jkl', v_row, blocks, precision=highest)
        keep = (rank_ids[None, :] < tile_rank[index][:, None]).astype(iterate.dtype)
        coeff = coeff * keep[:, :, None]
        u_row = lax.dynamic_slice_in_dim(u_basis, index * R_DEV, R_DEV, 2)
        return jnp.einsum('jkr,jkl->rl', u_row, coeff, precision=highest)

    far = lax.map(tile_row, jnp.arange(TILES, dtype=jnp.int32)).reshape(N, LOADS)
    near = jnp.einsum('prs,psl->prl', near_block.reshape(TILES, R_DEV, R_DEV), blocks, precision=highest).reshape(N, LOADS)
    residual = rhs - (fem + (far + near))
    updated = iterate + precond[:, None] * residual
    return updated, residual
```

```python
import functools
import math

import jax
import jax.numpy as jnp
from jax import lax
from jax.experimental import pallas as pl
from jax.experimental.pallas import tpu as pltpu
from jax.sharding import PartitionSpec as P

MESH = pl.DeviceIdType.MESH
F32 = jnp.float32
BF16 = jnp.bfloat16


def halves(x):
    high = x.astype(BF16)
    low = (x - high.astype(F32)).astype(BF16)
    return high, low


def mm(a, b):
    return jnp.dot(a, b, preferred_element_type=F32)


def pair(x):
    high, low = halves(x)
    return jnp.concatenate([high, low], axis=1), high


def fold(p):
    width = p.shape[1] // 2
    return p[:, :width] + p[:, width:]


def product(a_high, a_low, b_both, b_high):
    return fold(mm(a_high, b_both)) + mm(a_low, b_high)


def kernel(
    n,
    iterate_hbm, schur_hbm, near_hbm, u_hbm, v_hbm, rank_hbm, rows_hbm, count_hbm,
    out_ref,
    iterate, schur, near, u, v, rank, rows, count,
    out_face, in_face, out_force, in_force, sent, gathered,
    u_high, u_low, s_high, s_low,
    load_sem, face_send, face_recv, force_send, force_recv, send_sem, recv_sem,
):
    me = lax.axis_index("wide")
    loads = iterate.shape[1]
    face = rows.shape[2]
    rank_top = v.shape[1]
    rows_here = iterate.shape[0]
    power = n & (n - 1) == 0
    bits = [1 << b for b in range(n.bit_length()) if 1 << b < n]
    flips = [bit * (1 - 2 * lax.rem(lax.div(me, bit), 2)) for bit in bits]

    def to_of(k):
        if power:
            return me + sum(flip for bit, flip in zip(bits, flips) if k & bit)
        return lax.rem(me + k, n)

    def from_of(k):
        return to_of(k) if power else lax.rem(me - k + n, n)

    barrier = pltpu.get_barrier_semaphore()
    for k in range(n - 1, 0, -1):
        pl.semaphore_signal(barrier, inc=1, device_id={"wide": to_of(k)}, device_id_type=MESH)

    names = {}
    order = (
        ("rows", rows_hbm, rows), ("count", count_hbm, count), ("iterate", iterate_hbm, iterate),
        ("rank", rank_hbm, rank), ("v", v_hbm, v), ("schur", schur_hbm, schur),
        ("u", u_hbm, u), ("near", near_hbm, near),
    )
    for at, (name, source, target) in enumerate(order):
        names[name] = pltpu.make_async_copy(source, target, load_sem.at[at])
        names[name].start()

    @pl.when(me == 0)
    def _():
        in_face[2] = jnp.zeros_like(in_face[2])
        in_force[0] = jnp.zeros_like(in_force[0])

    @pl.when(me == n - 1)
    def _():
        in_face[0] = jnp.zeros_like(in_face[0])
        in_force[2] = jnp.zeros_like(in_force[2])

    names["rows"].wait()
    names["count"].wait()
    slot_ids = lax.broadcasted_iota(jnp.int32, (1, face), 1)
    row_of = []
    for o in range(3):
        row_of.append(jnp.where(slot_ids < count[0, o], rows[o], -1))
    names["iterate"].wait()
    it_both, it_high = pair(iterate[...])
    lanes = lax.broadcasted_iota(jnp.int32, (face, rows_here), 1)
    for o in (0, 2, 1):
        column = jnp.broadcast_to(row_of[o].astype(F32), (face, face)).T[:, :1].astype(jnp.int32)
        select = (column == lanes).astype(F32).astype(BF16)
        picked = fold(mm(select, it_both))
        if o == 1:
            in_face[1] = picked
        else:
            out_face[o // 2] = picked

    names["rank"].wait()
    names["v"].wait()
    group = math.gcd(n, max(1, 128 // rank_top))
    rank_ids = lax.broadcasted_iota(jnp.int32, (rank_top, loads), 0)
    for first in range(n - group, -1, -group):
        block = jnp.concatenate([v[to_of(first + g)] for g in range(group)], axis=0)
        v_high, v_low = halves(block)
        coeff = product(v_high, v_low, it_both, it_high)
        for g in range(group):
            part = coeff[g * rank_top : (g + 1) * rank_top]
            part = jnp.where(rank_ids < rank[0, to_of(first + g)], part, 0.0)
            if first + g == 0:
                gathered[0] = part
            else:
                sent[first + g] = part

    pl.semaphore_wait(barrier, n - 1)

    def face_copy(o, source, target, send, recv, peer):
        return pltpu.make_async_remote_copy(
            src_ref=source, dst_ref=target, send_sem=send.at[o // 2], recv_sem=recv.at[o // 2],
            device_id={"wide": peer}, device_id_type=MESH,
        )

    below, above = lax.rem(me + n - 1, n), lax.rem(me + 1, n)
    faces = {
        0: face_copy(0, out_face.at[0], in_face.at[0], face_send, face_recv, below),
        2: face_copy(2, out_face.at[1], in_face.at[2], face_send, face_recv, above),
    }
    returns = {
        0: face_copy(0, out_force.at[0], in_force.at[0], force_send, force_recv, above),
        2: face_copy(2, out_force.at[1], in_force.at[2], force_send, force_recv, below),
    }
    has_below, has_above = me > 0, me < n - 1

    @pl.when(has_below)
    def _():
        faces[0].start()

    @pl.when(has_above)
    def _():
        faces[2].start()

    copies = {}
    for k in range(n - 1, 0, -1):
        copies[k] = pltpu.make_async_remote_copy(
            src_ref=sent.at[k], dst_ref=gathered.at[k], send_sem=send_sem.at[k], recv_sem=recv_sem.at[k],
            device_id={"wide": to_of(k)}, device_id_type=MESH,
        )
        copies[k].start()

    names["schur"].wait()
    high, low = halves(schur[0])
    s_high[...] = high
    s_low[...] = low
    mid = slice(face, 2 * face)
    b_both, b_high = pair(in_face[1])
    force = product(s_high[:, mid], s_low[:, mid], b_both, b_high)
    names["u"].wait()
    names["near"].wait()
    for first in range(0, n, group):
        block = jnp.concatenate([u[from_of(first + g)] for g in range(group)], axis=0).T
        high, low = halves(block)
        u_high[:, first * rank_top : (first + group) * rank_top] = high
        u_low[:, first * rank_top : (first + group) * rank_top] = low
    near_high, near_low = halves(near[...])
    out_ref[...] = product(near_high, near_low, it_both, it_high)

    @pl.when(has_above)
    def _():
        faces[0].wait_recv()

    @pl.when(has_below)
    def _():
        faces[2].wait_recv()

    for o in (0, 2):
        span = slice(o * face, (o + 1) * face)
        b_both, b_high = pair(in_face[o])
        force = force + product(s_high[:, span], s_low[:, span], b_both, b_high)
    out_force[0] = force[:face]
    out_force[1] = force[2 * face :]
    in_force[1] = force[mid]

    @pl.when(has_above)
    def _():
        returns[0].start()

    @pl.when(has_below)
    def _():
        returns[2].start()

    def far(first, size):
        for k in range(max(first, 1), first + size):
            copies[k].wait_recv()
        got = gathered[first : first + size].reshape(size * rank_top, loads)
        b_both, b_high = pair(got)
        span = slice(first * rank_top, (first + size) * rank_top)
        return product(u_high[:, span], u_low[:, span], b_both, b_high)

    chunk = math.gcd(n, 2 * group)
    for first in range(0, n - chunk, chunk):
        out_ref[...] += far(first, chunk)

    @pl.when(has_below)
    def _():
        returns[0].wait_recv()

    @pl.when(has_above)
    def _():
        returns[2].wait_recv()

    total = out_ref[...]
    place = lax.broadcasted_iota(jnp.int32, (rows_here, face), 0)
    for o in range(3):
        scatter = (place == row_of[o]).astype(F32).astype(BF16)
        b_both, _ = pair(in_force[o])
        total = total + fold(mm(scatter, b_both))
    total = total + far(n - chunk, chunk)
    out_ref[...] = total

    @pl.when(has_below)
    def _():
        faces[0].wait_send()
        returns[2].wait_send()

    @pl.when(has_above)
    def _():
        faces[2].wait_send()
        returns[0].wait_send()

    for k in range(1, n):
        copies[k].wait_send()


def body(
    iterate, rhs, schur, near_block, u_basis, v_basis, tile_rank, send_rows, send_count, precond
):
    n = lax.axis_size("wide")
    rows_here, loads = iterate.shape
    face = send_rows.shape[2]
    tiles, rank_top, _ = u_basis.shape
    tile_rank = tile_rank.reshape(1, tiles)
    send_rows = send_rows.reshape(3, 1, face)
    dma = pltpu.SemaphoreType.DMA
    applied = pl.pallas_call(
        functools.partial(kernel, n),
        out_shape=pltpu.VMEM((rows_here, loads), F32),
        in_specs=[pl.BlockSpec(memory_space=pl.ANY)] * 8,
        out_specs=pl.BlockSpec(memory_space=pltpu.VMEM),
        scratch_shapes=[
            pltpu.VMEM(iterate.shape, F32),
            pltpu.VMEM(schur.shape, F32),
            pltpu.VMEM(near_block.shape, F32),
            pltpu.VMEM(u_basis.shape, F32),
            pltpu.VMEM(v_basis.shape, F32),
            pltpu.SMEM(tile_rank.shape, jnp.int32),
            pltpu.VMEM(send_rows.shape, jnp.int32),
            pltpu.SMEM(send_count.shape, jnp.int32),
            pltpu.VMEM((2, face, loads), F32),
            pltpu.VMEM((3, face, loads), F32),
            pltpu.VMEM((2, face, loads), F32),
            pltpu.VMEM((3, face, loads), F32),
            pltpu.VMEM((n, rank_top, loads), F32),
            pltpu.VMEM((n, rank_top, loads), F32),
            pltpu.VMEM((rows_here, tiles * rank_top), BF16),
            pltpu.VMEM((rows_here, tiles * rank_top), BF16),
            pltpu.VMEM(schur.shape[1:], BF16),
            pltpu.VMEM(schur.shape[1:], BF16),
            dma((8,)),
            dma((2,)),
            dma((2,)),
            dma((2,)),
            dma((2,)),
            dma((n,)),
            dma((n,)),
        ],
        compiler_params=pltpu.CompilerParams(collective_id=0, has_side_effects=True),
    )(iterate, schur, near_block, u_basis, v_basis, tile_rank, send_rows, send_count)
    residual = rhs - applied
    updated = iterate + precond[:, None] * residual
    return (updated, residual)


def solution(mesh):
    in_specs = (
        P(("groups", "wide"), None),
        P(("groups", "wide"), None),
        P(("groups", "wide"), None, None),
        P(("groups", "wide"), None),
        P("groups", None, "wide"),
        P("groups", None, "wide"),
        P("groups", "wide"),
        P(("groups", "wide"), None, None),
        P(("groups", "wide"), None),
        P(("groups", "wide")),
    )
    out_specs = (P(("groups", "wide"), None), P(("groups", "wide"), None))
    return jax.shard_map(body, mesh=mesh, in_specs=in_specs, out_specs=out_specs, check_vma=False)
```

```python
import functools
import math

import jax
import jax.numpy as jnp
from jax import lax
from jax.experimental import pallas as pl
from jax.experimental.pallas import tpu as pltpu
from jax.sharding import PartitionSpec as P

EARLY = 2
STRIDE = False
FIRST = 0
JOIN = 0
TAIL = 1
MESH = pl.DeviceIdType.MESH
F32 = jnp.float32
BF16 = jnp.bfloat16


def halves(x):
    high = x.astype(BF16)
    low = (x - high.astype(F32)).astype(BF16)
    return high, low


def mm(a, b):
    return jnp.dot(a, b, preferred_element_type=F32)


def pair(x):
    high, low = halves(x)
    return jnp.concatenate([high, low], axis=1), high


def fold(p):
    width = p.shape[1] // 2
    return p[:, :width] + p[:, width:]


def product(a_high, a_low, b_both, b_high):
    return fold(mm(a_high, b_both)) + mm(a_low, b_high)


def kernel(
    n,
    iterate_hbm, schur_hbm, near_hbm, u_hbm, v_hbm, rank_hbm, rows_hbm, count_hbm,
    out_ref,
    iterate, schur, near, u, v, rank, rows, count,
    out_face, in_face, out_force, in_force, sent, gathered,
    u_high, u_low, s_high, s_low,
    load_sem, face_send, face_recv, force_send, force_recv, send_sem, recv_sem,
):
    me = lax.axis_index("wide")
    loads = iterate.shape[1]
    face = rows.shape[2]
    rank_top = v.shape[1]
    rows_here = iterate.shape[0]
    power = n & (n - 1) == 0
    bits = [1 << b for b in range(n.bit_length()) if 1 << b < n]
    flips = [bit * (1 - 2 * lax.rem(lax.div(me, bit), 2)) for bit in bits]

    def to_of(k):
        if power:
            return me + sum(flip for bit, flip in zip(bits, flips) if k & bit)
        return lax.rem(me + k, n)

    def from_of(k):
        return to_of(k) if power else lax.rem(me - k + n, n)

    barrier = pltpu.get_barrier_semaphore()
    for k in range(n - 1, 0, -1):
        pl.semaphore_signal(barrier, inc=1, device_id={"wide": to_of(k)}, device_id_type=MESH)

    group = math.gcd(n, max(1, 128 // rank_top))
    if STRIDE:
        groups = [[step + n // group * g for g in range(group - 1, -1, -1)] for step in range(n // group - 1, -1, -1)]
    else:
        groups = [[first + g for g in range(group - 1, -1, -1)] for first in range(n - group, -1, -group)]
    slot_of = {k: at for at, k in enumerate(k for members in groups for k in members)}

    names = {}
    def load(name, at, source, target):
        names[name] = pltpu.make_async_copy(source, target, load_sem.at[at])
        names[name].start()

    load("iterate", 0, iterate_hbm, iterate)
    load("rank", 1, rank_hbm, rank)
    for at, k in enumerate(slot_of):
        if at < group:
            load(k, 7 + at, v_hbm.at[to_of(k)], v.at[at])
    load("rows", 2, rows_hbm, rows)
    load("count", 3, count_hbm, count)
    for at, k in enumerate(slot_of):
        if at >= group:
            load(k, 7 + at, v_hbm.at[to_of(k)], v.at[at])
    load("schur", 4, schur_hbm, schur)
    load("u", 5, u_hbm, u)
    load("near", 6, near_hbm, near)

    @pl.when(me == 0)
    def _():
        in_face[2] = jnp.zeros_like(in_face[2])
        in_force[0] = jnp.zeros_like(in_force[0])

    @pl.when(me == n - 1)
    def _():
        in_face[0] = jnp.zeros_like(in_face[0])
        in_force[2] = jnp.zeros_like(in_force[2])

    names["iterate"].wait()
    it_both, it_high = pair(iterate[...])
    rank_ids = lax.broadcasted_iota(jnp.int32, (rank_top, loads), 0)
    copies = {
        k: pltpu.make_async_remote_copy(
            src_ref=sent.at[slot], dst_ref=gathered.at[slot], send_sem=send_sem.at[slot],
            recv_sem=recv_sem.at[slot], device_id={"wide": to_of(k)}, device_id_type=MESH,
        )
        for k, slot in slot_of.items() if k > 0
    }

    def compress(members):
        for k in members:
            names[k].wait()
        block = jnp.concatenate([v[slot_of[k]] for k in members], axis=0)
        v_high, v_low = halves(block)
        coeff = product(v_high, v_low, it_both, it_high)
        for g, k in enumerate(members):
            part = coeff[g * rank_top : (g + 1) * rank_top]
            part = jnp.where(rank_ids < rank[0, to_of(k)], part, 0.0)
            if k == 0:
                gathered[slot_of[k]] = part
            else:
                sent[slot_of[k]] = part

    def send(members):
        for k in members:
            if k > 0:
                copies[k].start()

    names["rank"].wait()
    early = min(EARLY, len(groups))
    for members in groups[:early]:
        compress(members)

    if FIRST:
        pl.semaphore_wait(barrier, n - 1)
        for members in groups[:early]:
            send(members)

    names["rows"].wait()
    names["count"].wait()
    slot_ids = lax.broadcasted_iota(jnp.int32, (1, face), 1)
    row_of = []
    for o in range(3):
        row_of.append(jnp.where(slot_ids < count[0, o], rows[o], -1))
    lanes = lax.broadcasted_iota(jnp.int32, (face, rows_here), 1)
    for o in (0, 2, 1):
        column = jnp.broadcast_to(row_of[o].astype(F32), (face, face)).T[:, :1].astype(jnp.int32)
        select = (column == lanes).astype(F32).astype(BF16)
        picked = fold(mm(select, it_both))
        if o == 1:
            in_face[1] = picked
        else:
            out_face[o // 2] = picked

    if not FIRST:
        pl.semaphore_wait(barrier, n - 1)

    def face_copy(o, source, target, send, recv, peer):
        return pltpu.make_async_remote_copy(
            src_ref=source, dst_ref=target, send_sem=send.at[o // 2], recv_sem=recv.at[o // 2],
            device_id={"wide": peer}, device_id_type=MESH,
        )

    below, above = lax.rem(me + n - 1, n), lax.rem(me + 1, n)
    faces = {
        0: face_copy(0, out_face.at[0], in_face.at[0], face_send, face_recv, below),
        2: face_copy(2, out_face.at[1], in_face.at[2], face_send, face_recv, above),
    }
    returns = {
        0: face_copy(0, out_force.at[0], in_force.at[0], force_send, force_recv, above),
        2: face_copy(2, out_force.at[1], in_force.at[2], force_send, force_recv, below),
    }
    has_below, has_above = me > 0, me < n - 1

    @pl.when(has_below)
    def _():
        faces[0].start()

    @pl.when(has_above)
    def _():
        faces[2].start()

    if not FIRST:
        for members in groups[:early]:
            send(members)
    for members in groups[early:]:
        compress(members)
        send(members)

    names["schur"].wait()
    high, low = halves(schur[0])
    s_high[...] = high
    s_low[...] = low
    mid = slice(face, 2 * face)
    b_both, b_high = pair(in_face[1])
    force = product(s_high[:, mid], s_low[:, mid], b_both, b_high)
    names["u"].wait()
    names["near"].wait()
    for at, members in enumerate(groups):
        block = jnp.concatenate([u[from_of(k)] for k in members], axis=0).T
        high, low = halves(block)
        span = slice(at * group * rank_top, (at + 1) * group * rank_top)
        u_high[:, span] = high
        u_low[:, span] = low
    near_high, near_low = halves(near[...])
    out_ref[...] = product(near_high, near_low, it_both, it_high)

    @pl.when(has_above)
    def _():
        faces[0].wait_recv()

    @pl.when(has_below)
    def _():
        faces[2].wait_recv()

    for o in (0, 2):
        span = slice(o * face, (o + 1) * face)
        b_both, b_high = pair(in_face[o])
        force = force + product(s_high[:, span], s_low[:, span], b_both, b_high)
    out_force[0] = force[:face]
    out_force[1] = force[2 * face :]
    in_force[1] = force[mid]

    @pl.when(has_above)
    def _():
        returns[0].start()

    @pl.when(has_below)
    def _():
        returns[2].start()

    def far(first, size):
        for k, slot in slot_of.items():
            if k > 0 and first <= slot < first + size:
                copies[k].wait_recv()
        got = gathered[first : first + size].reshape(size * rank_top, loads)
        b_both, b_high = pair(got)
        span = slice(first * rank_top, (first + size) * rank_top)
        return product(u_high[:, span], u_low[:, span], b_both, b_high)

    spans = [(at * group, group) for at in range(len(groups))]
    half = len(spans) // 2
    spans = spans[half:][::-1] + spans[:half]
    if JOIN and half > 1:
        spans = spans[:-half] + [(at * group, 2 * group) for at in range(0, half - 1, 2)]
        if half % 2:
            spans = spans[:-1] + [((half - 1) * group, group), spans[-1]]
    for first, size in spans[: len(spans) - TAIL]:
        out_ref[...] += far(first, size)

    @pl.when(has_below)
    def _():
        returns[0].wait_recv()

    @pl.when(has_above)
    def _():
        returns[2].wait_recv()

    total = out_ref[...]
    place = lax.broadcasted_iota(jnp.int32, (rows_here, face), 0)
    for o in range(3):
        scatter = (place == row_of[o]).astype(F32).astype(BF16)
        b_both, _ = pair(in_force[o])
        total = total + fold(mm(scatter, b_both))
    for first, size in spans[len(spans) - TAIL :]:
        total = total + far(first, size)
    out_ref[...] = total

    @pl.when(has_below)
    def _():
        faces[0].wait_send()
        returns[2].wait_send()

    @pl.when(has_above)
    def _():
        faces[2].wait_send()
        returns[0].wait_send()

    for k in range(1, n):
        copies[k].wait_send()


def body(
    iterate, rhs, schur, near_block, u_basis, v_basis, tile_rank, send_rows, send_count, precond
):
    n = lax.axis_size("wide")
    rows_here, loads = iterate.shape
    face = send_rows.shape[2]
    tiles, rank_top, _ = u_basis.shape
    tile_rank = tile_rank.reshape(1, tiles)
    send_rows = send_rows.reshape(3, 1, face)
    dma = pltpu.SemaphoreType.DMA
    applied = pl.pallas_call(
        functools.partial(kernel, n),
        out_shape=pltpu.VMEM((rows_here, loads), F32),
        in_specs=[pl.BlockSpec(memory_space=pl.ANY)] * 8,
        out_specs=pl.BlockSpec(memory_space=pltpu.VMEM),
        scratch_shapes=[
            pltpu.VMEM(iterate.shape, F32),
            pltpu.VMEM(schur.shape, F32),
            pltpu.VMEM(near_block.shape, F32),
            pltpu.VMEM(u_basis.shape, F32),
            pltpu.VMEM(v_basis.shape, F32),
            pltpu.SMEM(tile_rank.shape, jnp.int32),
            pltpu.VMEM(send_rows.shape, jnp.int32),
            pltpu.SMEM(send_count.shape, jnp.int32),
            pltpu.VMEM((2, face, loads), F32),
            pltpu.VMEM((3, face, loads), F32),
            pltpu.VMEM((2, face, loads), F32),
            pltpu.VMEM((3, face, loads), F32),
            pltpu.VMEM((n, rank_top, loads), F32),
            pltpu.VMEM((n, rank_top, loads), F32),
            pltpu.VMEM((rows_here, tiles * rank_top), BF16),
            pltpu.VMEM((rows_here, tiles * rank_top), BF16),
            pltpu.VMEM(schur.shape[1:], BF16),
            pltpu.VMEM(schur.shape[1:], BF16),
            dma((7 + n,)),
            dma((2,)),
            dma((2,)),
            dma((2,)),
            dma((2,)),
            dma((n,)),
            dma((n,)),
        ],
        compiler_params=pltpu.CompilerParams(collective_id=0, has_side_effects=True),
    )(iterate, schur, near_block, u_basis, v_basis, tile_rank, send_rows, send_count)
    residual = rhs - applied
    updated = iterate + precond[:, None] * residual
    return (updated, residual)


def solution(mesh):
    in_specs = (
        P(("groups", "wide"), None),
        P(("groups", "wide"), None),
        P(("groups", "wide"), None, None),
        P(("groups", "wide"), None),
        P("groups", None, "wide"),
        P("groups", None, "wide"),
        P("groups", "wide"),
        P(("groups", "wide"), None, None),
        P(("groups", "wide"), None),
        P(("groups", "wide")),
    )
    out_specs = (P(("groups", "wide"), None), P(("groups", "wide"), None))
    return jax.shard_map(body, mesh=mesh, in_specs=in_specs, out_specs=out_specs, check_vma=False)
```

```python
import functools
import math

import jax
import jax.numpy as jnp
from jax import lax
from jax.experimental import pallas as pl
from jax.experimental.pallas import tpu as pltpu
from jax.sharding import PartitionSpec as P

EARLY = 2
STRIDE = False
FIRST = 0
JOIN = 0
TAIL = 1
MESH = pl.DeviceIdType.MESH
F32 = jnp.float32
BF16 = jnp.bfloat16


def halves(x):
    high = x.astype(BF16)
    low = (x - high.astype(F32)).astype(BF16)
    return high, low


def mm(a, b):
    return jnp.dot(a, b, preferred_element_type=F32)


def pair(x):
    high, low = halves(x)
    return jnp.concatenate([high, low], axis=1), high


def fold(p):
    width = p.shape[1] // 2
    return p[:, :width] + p[:, width:]


def product(a_high, a_low, b_both, b_high):
    return fold(mm(a_high, b_both)) + mm(a_low, b_high)


def kernel(
    n,
    iterate_hbm, schur_hbm, near_hbm, u_hbm, v_hbm, rank_hbm, rows_hbm, count_hbm,
    out_ref,
    iterate, schur, near, u, v, rank, rows, count,
    out_face, in_face, out_force, in_force, sent, gathered,
    u_high, u_low, s_high, s_low,
    load_sem, face_send, face_recv, force_send, force_recv, send_sem, recv_sem,
):
    me = lax.axis_index("wide")
    loads = iterate.shape[1]
    face = rows.shape[2]
    rank_top = v.shape[1]
    rows_here = iterate.shape[0]
    power = n & (n - 1) == 0
    bits = [1 << b for b in range(n.bit_length()) if 1 << b < n]
    flips = [bit * (1 - 2 * lax.rem(lax.div(me, bit), 2)) for bit in bits]

    def to_of(k):
        if power:
            return me + sum(flip for bit, flip in zip(bits, flips) if k & bit)
        return lax.rem(me + k, n)

    def from_of(k):
        return to_of(k) if power else lax.rem(me - k + n, n)

    barrier = pltpu.get_barrier_semaphore()
    for k in range(n - 1, 0, -1):
        pl.semaphore_signal(barrier, inc=1, device_id={"wide": to_of(k)}, device_id_type=MESH)

    group = math.gcd(n, max(1, 128 // rank_top))
    if STRIDE:
        groups = [[step + n // group * g for g in range(group - 1, -1, -1)] for step in range(n // group - 1, -1, -1)]
    else:
        groups = [[first + g for g in range(group)] for first in range(n - group, -1, -group)]
    slot_of = {k: at for at, k in enumerate(k for members in groups for k in members)}

    names = {}
    def load(name, at, source, target):
        names[name] = pltpu.make_async_copy(source, target, load_sem.at[at])
        names[name].start()

    load("iterate", 0, iterate_hbm, iterate)
    load("rank", 1, rank_hbm, rank)
    for at, k in enumerate(slot_of):
        if at < group:
            load(k, 7 + at, v_hbm.at[to_of(k)], v.at[at])
    load("rows", 2, rows_hbm, rows)
    load("count", 3, count_hbm, count)
    for at, k in enumerate(slot_of):
        if at >= group:
            load(k, 7 + at, v_hbm.at[to_of(k)], v.at[at])
    load("schur", 4, schur_hbm, schur)
    load("u", 5, u_hbm, u)
    load("near", 6, near_hbm, near)

    @pl.when(me == 0)
    def _():
        in_face[2] = jnp.zeros_like(in_face[2])
        in_force[0] = jnp.zeros_like(in_force[0])

    @pl.when(me == n - 1)
    def _():
        in_face[0] = jnp.zeros_like(in_face[0])
        in_force[2] = jnp.zeros_like(in_force[2])

    names["iterate"].wait()
    it_both, it_high = pair(iterate[...])
    rank_ids = lax.broadcasted_iota(jnp.int32, (rank_top, loads), 0)
    copies = {
        k: pltpu.make_async_remote_copy(
            src_ref=sent.at[slot], dst_ref=gathered.at[slot], send_sem=send_sem.at[slot],
            recv_sem=recv_sem.at[slot], device_id={"wide": to_of(k)}, device_id_type=MESH,
        )
        for k, slot in slot_of.items() if k > 0
    }

    def compress(members):
        for k in members:
            names[k].wait()
        block = jnp.concatenate([v[slot_of[k]] for k in members], axis=0)
        v_high, v_low = halves(block)
        coeff = product(v_high, v_low, it_both, it_high)
        for g, k in enumerate(members):
            part = coeff[g * rank_top : (g + 1) * rank_top]
            part = jnp.where(rank_ids < rank[0, to_of(k)], part, 0.0)
            if k == 0:
                gathered[slot_of[k]] = part
            else:
                sent[slot_of[k]] = part

    def send(members):
        for k in members:
            if k > 0:
                copies[k].start()

    names["rank"].wait()
    early = min(EARLY, len(groups))
    for members in groups[:early]:
        compress(members)

    if FIRST:
        pl.semaphore_wait(barrier, n - 1)
        for members in groups[:early]:
            send(members)

    names["rows"].wait()
    names["count"].wait()
    slot_ids = lax.broadcasted_iota(jnp.int32, (1, face), 1)
    row_of = []
    for o in range(3):
        row_of.append(jnp.where(slot_ids < count[0, o], rows[o], -1))
    lanes = lax.broadcasted_iota(jnp.int32, (face, rows_here), 1)
    for o in (0, 2, 1):
        column = jnp.broadcast_to(row_of[o].astype(F32), (face, face)).T[:, :1].astype(jnp.int32)
        select = (column == lanes).astype(F32).astype(BF16)
        picked = fold(mm(select, it_both))
        if o == 1:
            in_face[1] = picked
        else:
            out_face[o // 2] = picked

    if not FIRST:
        pl.semaphore_wait(barrier, n - 1)

    def face_copy(o, source, target, send, recv, peer):
        return pltpu.make_async_remote_copy(
            src_ref=source, dst_ref=target, send_sem=send.at[o // 2], recv_sem=recv.at[o // 2],
            device_id={"wide": peer}, device_id_type=MESH,
        )

    below, above = lax.rem(me + n - 1, n), lax.rem(me + 1, n)
    faces = {
        0: face_copy(0, out_face.at[0], in_face.at[0], face_send, face_recv, below),
        2: face_copy(2, out_face.at[1], in_face.at[2], face_send, face_recv, above),
    }
    returns = {
        0: face_copy(0, out_force.at[0], in_force.at[0], force_send, force_recv, above),
        2: face_copy(2, out_force.at[1], in_force.at[2], force_send, force_recv, below),
    }
    has_below, has_above = me > 0, me < n - 1

    @pl.when(has_below)
    def _():
        faces[0].start()

    @pl.when(has_above)
    def _():
        faces[2].start()

    if not FIRST:
        for members in groups[:early]:
            send(members)
    for members in groups[early:]:
        compress(members)
        send(members)

    names["schur"].wait()
    high, low = halves(schur[0])
    s_high[...] = high
    s_low[...] = low
    mid = slice(face, 2 * face)
    b_both, b_high = pair(in_face[1])
    force = product(s_high[:, mid], s_low[:, mid], b_both, b_high)
    @pl.when(has_above)
    def _():
        faces[0].wait_recv()

    @pl.when(has_below)
    def _():
        faces[2].wait_recv()

    for o in (0, 2):
        span = slice(o * face, (o + 1) * face)
        b_both, b_high = pair(in_face[o])
        force = force + product(s_high[:, span], s_low[:, span], b_both, b_high)
    out_force[0] = force[:face]
    out_force[1] = force[2 * face :]
    in_force[1] = force[mid]

    @pl.when(has_above)
    def _():
        returns[0].start()

    @pl.when(has_below)
    def _():
        returns[2].start()

    names["u"].wait()
    names["near"].wait()
    for at, members in enumerate(groups):
        block = jnp.concatenate([u[from_of(k)] for k in members], axis=0).T
        high, low = halves(block)
        span = slice(at * group * rank_top, (at + 1) * group * rank_top)
        u_high[:, span] = high
        u_low[:, span] = low
    near_high, near_low = halves(near[...])
    out_ref[...] = product(near_high, near_low, it_both, it_high)

    def far(first, size):
        for k, slot in slot_of.items():
            if k > 0 and first <= slot < first + size:
                copies[k].wait_recv()
        got = gathered[first : first + size].reshape(size * rank_top, loads)
        b_both, b_high = pair(got)
        span = slice(first * rank_top, (first + size) * rank_top)
        return product(u_high[:, span], u_low[:, span], b_both, b_high)

    spans = [(at * group, group) for at in range(len(groups))]
    half = len(spans) // 2
    spans = spans[half:][::-1] + spans[:half]
    if JOIN and half > 1:
        spans = spans[:-half] + [(at * group, 2 * group) for at in range(0, half - 1, 2)]
        if half % 2:
            spans = spans[:-1] + [((half - 1) * group, group), spans[-1]]
    for first, size in spans[: len(spans) - TAIL]:
        out_ref[...] += far(first, size)

    @pl.when(has_below)
    def _():
        returns[0].wait_recv()

    @pl.when(has_above)
    def _():
        returns[2].wait_recv()

    total = out_ref[...]
    place = lax.broadcasted_iota(jnp.int32, (rows_here, face), 0)
    for o in range(3):
        scatter = (place == row_of[o]).astype(F32).astype(BF16)
        b_both, _ = pair(in_force[o])
        total = total + fold(mm(scatter, b_both))
    for first, size in spans[len(spans) - TAIL :]:
        total = total + far(first, size)
    out_ref[...] = total

    @pl.when(has_below)
    def _():
        faces[0].wait_send()
        returns[2].wait_send()

    @pl.when(has_above)
    def _():
        faces[2].wait_send()
        returns[0].wait_send()

    for k in range(1, n):
        copies[k].wait_send()


def body(
    iterate, rhs, schur, near_block, u_basis, v_basis, tile_rank, send_rows, send_count, precond
):
    n = lax.axis_size("wide")
    rows_here, loads = iterate.shape
    face = send_rows.shape[2]
    tiles, rank_top, _ = u_basis.shape
    tile_rank = tile_rank.reshape(1, tiles)
    send_rows = send_rows.reshape(3, 1, face)
    dma = pltpu.SemaphoreType.DMA
    applied = pl.pallas_call(
        functools.partial(kernel, n),
        out_shape=pltpu.VMEM((rows_here, loads), F32),
        in_specs=[pl.BlockSpec(memory_space=pl.ANY)] * 8,
        out_specs=pl.BlockSpec(memory_space=pltpu.VMEM),
        scratch_shapes=[
            pltpu.VMEM(iterate.shape, F32),
            pltpu.VMEM(schur.shape, F32),
            pltpu.VMEM(near_block.shape, F32),
            pltpu.VMEM(u_basis.shape, F32),
            pltpu.VMEM(v_basis.shape, F32),
            pltpu.SMEM(tile_rank.shape, jnp.int32),
            pltpu.VMEM(send_rows.shape, jnp.int32),
            pltpu.SMEM(send_count.shape, jnp.int32),
            pltpu.VMEM((2, face, loads), F32),
            pltpu.VMEM((3, face, loads), F32),
            pltpu.VMEM((2, face, loads), F32),
            pltpu.VMEM((3, face, loads), F32),
            pltpu.VMEM((n, rank_top, loads), F32),
            pltpu.VMEM((n, rank_top, loads), F32),
            pltpu.VMEM((rows_here, tiles * rank_top), BF16),
            pltpu.VMEM((rows_here, tiles * rank_top), BF16),
            pltpu.VMEM(schur.shape[1:], BF16),
            pltpu.VMEM(schur.shape[1:], BF16),
            dma((7 + n,)),
            dma((2,)),
            dma((2,)),
            dma((2,)),
            dma((2,)),
            dma((n,)),
            dma((n,)),
        ],
        compiler_params=pltpu.CompilerParams(collective_id=0, has_side_effects=True),
    )(iterate, schur, near_block, u_basis, v_basis, tile_rank, send_rows, send_count)
    residual = rhs - applied
    updated = iterate + precond[:, None] * residual
    return (updated, residual)


def solution(mesh):
    in_specs = (
        P(("groups", "wide"), None),
        P(("groups", "wide"), None),
        P(("groups", "wide"), None, None),
        P(("groups", "wide"), None),
        P("groups", None, "wide"),
        P("groups", None, "wide"),
        P("groups", "wide"),
        P(("groups", "wide"), None, None),
        P(("groups", "wide"), None),
        P(("groups", "wide")),
    )
    out_specs = (P(("groups", "wide"), None), P(("groups", "wide"), None))
    return jax.shard_map(body, mesh=mesh, in_specs=in_specs, out_specs=out_specs, check_vma=False)
```

```python
import functools
import math

import jax
import jax.numpy as jnp
from jax import lax
from jax.experimental import pallas as pl
from jax.experimental.pallas import tpu as pltpu
from jax.sharding import PartitionSpec as P

EARLY = 2
STRIDE = False
FIRST = 0
JOIN = 0
TAIL = 1
MESH = pl.DeviceIdType.MESH
F32 = jnp.float32
BF16 = jnp.bfloat16


def halves(x):
    high = x.astype(BF16)
    low = (x - high.astype(F32)).astype(BF16)
    return high, low


def mm(a, b):
    return jnp.dot(a, b, preferred_element_type=F32)


def pair(x):
    high, low = halves(x)
    return jnp.concatenate([high, low], axis=1), high


def fold(p):
    width = p.shape[1] // 2
    return p[:, :width] + p[:, width:]


def product(a_high, a_low, b_both, b_high):
    return fold(mm(a_high, b_both)) + mm(a_low, b_high)


def kernel(
    n,
    iterate_hbm, schur_hbm, near_hbm, u_hbm, v_hbm, rank_hbm, rows_hbm, count_hbm,
    out_ref,
    iterate, schur, near, u, v, rank, rows, count,
    out_face, in_face, out_force, in_force, sent, gathered,
    u_high, u_low, s_high, s_low,
    load_sem, face_send, face_recv, force_send, force_recv, send_sem, recv_sem,
):
    me = lax.axis_index("wide")
    loads = iterate.shape[1]
    face = rows.shape[2]
    rank_top = v.shape[1]
    rows_here = iterate.shape[0]
    power = n & (n - 1) == 0
    bits = [1 << b for b in range(n.bit_length()) if 1 << b < n]
    flips = [bit * (1 - 2 * lax.rem(lax.div(me, bit), 2)) for bit in bits]

    def to_of(k):
        if power:
            return me + sum(flip for bit, flip in zip(bits, flips) if k & bit)
        return lax.rem(me + k, n)

    def from_of(k):
        return to_of(k) if power else lax.rem(me - k + n, n)

    barrier = pltpu.get_barrier_semaphore()
    for k in range(n - 1, 0, -1):
        pl.semaphore_signal(barrier, inc=1, device_id={"wide": to_of(k)}, device_id_type=MESH)

    group = math.gcd(n, max(1, 128 // rank_top))
    if STRIDE:
        groups = [[step + n // group * g for g in range(group - 1, -1, -1)] for step in range(n // group - 1, -1, -1)]
    else:
        halfway = n // 2 // group * group
        firsts = [*range(halfway, n - group + 1, group), *range(halfway - group, -1, -group)]
        groups = [[first + g for g in range(group)] for first in firsts]
    slot_of = {k: at for at, k in enumerate(k for members in groups for k in members)}

    names = {}
    def load(name, at, source, target):
        names[name] = pltpu.make_async_copy(source, target, load_sem.at[at])
        names[name].start()

    load("iterate", 0, iterate_hbm, iterate)
    load("rank", 1, rank_hbm, rank)
    for at, k in enumerate(slot_of):
        if at < group:
            load(k, 7 + at, v_hbm.at[to_of(k)], v.at[at])
    load("rows", 2, rows_hbm, rows)
    load("count", 3, count_hbm, count)
    for at, k in enumerate(slot_of):
        if at >= group:
            load(k, 7 + at, v_hbm.at[to_of(k)], v.at[at])
    load("schur", 4, schur_hbm, schur)
    load("u", 5, u_hbm, u)
    load("near", 6, near_hbm, near)

    @pl.when(me == 0)
    def _():
        in_face[2] = jnp.zeros_like(in_face[2])
        in_force[0] = jnp.zeros_like(in_force[0])

    @pl.when(me == n - 1)
    def _():
        in_face[0] = jnp.zeros_like(in_face[0])
        in_force[2] = jnp.zeros_like(in_force[2])

    names["iterate"].wait()
    it_both, it_high = pair(iterate[...])
    rank_ids = lax.broadcasted_iota(jnp.int32, (rank_top, loads), 0)
    copies = {
        k: pltpu.make_async_remote_copy(
            src_ref=sent.at[slot], dst_ref=gathered.at[slot], send_sem=send_sem.at[slot],
            recv_sem=recv_sem.at[slot], device_id={"wide": to_of(k)}, device_id_type=MESH,
        )
        for k, slot in slot_of.items() if k > 0
    }

    def compress(members):
        for k in members:
            names[k].wait()
        block = jnp.concatenate([v[slot_of[k]] for k in members], axis=0)
        v_high, v_low = halves(block)
        coeff = product(v_high, v_low, it_both, it_high)
        for g, k in enumerate(members):
            part = coeff[g * rank_top : (g + 1) * rank_top]
            part = jnp.where(rank_ids < rank[0, to_of(k)], part, 0.0)
            if k == 0:
                gathered[slot_of[k]] = part
            else:
                sent[slot_of[k]] = part

    def send(members):
        for k in members:
            if k > 0:
                copies[k].start()

    names["rank"].wait()
    early = min(EARLY, len(groups))
    for members in groups[:early]:
        compress(members)

    if FIRST:
        pl.semaphore_wait(barrier, n - 1)
        for members in groups[:early]:
            send(members)

    names["rows"].wait()
    names["count"].wait()
    slot_ids = lax.broadcasted_iota(jnp.int32, (1, face), 1)
    row_of = []
    for o in range(3):
        row_of.append(jnp.where(slot_ids < count[0, o], rows[o], -1))
    lanes = lax.broadcasted_iota(jnp.int32, (face, rows_here), 1)
    for o in (0, 2, 1):
        column = jnp.broadcast_to(row_of[o].astype(F32), (face, face)).T[:, :1].astype(jnp.int32)
        select = (column == lanes).astype(F32).astype(BF16)
        picked = fold(mm(select, it_both))
        if o == 1:
            in_face[1] = picked
        else:
            out_face[o // 2] = picked

    if not FIRST:
        pl.semaphore_wait(barrier, n - 1)

    def face_copy(o, source, target, send, recv, peer):
        return pltpu.make_async_remote_copy(
            src_ref=source, dst_ref=target, send_sem=send.at[o // 2], recv_sem=recv.at[o // 2],
            device_id={"wide": peer}, device_id_type=MESH,
        )

    below, above = lax.rem(me + n - 1, n), lax.rem(me + 1, n)
    faces = {
        0: face_copy(0, out_face.at[0], in_face.at[0], face_send, face_recv, below),
        2: face_copy(2, out_face.at[1], in_face.at[2], face_send, face_recv, above),
    }
    returns = {
        0: face_copy(0, out_force.at[0], in_force.at[0], force_send, force_recv, above),
        2: face_copy(2, out_force.at[1], in_force.at[2], force_send, force_recv, below),
    }
    has_below, has_above = me > 0, me < n - 1

    @pl.when(has_below)
    def _():
        faces[0].start()

    @pl.when(has_above)
    def _():
        faces[2].start()

    if not FIRST:
        for members in groups[:early]:
            send(members)
    for members in groups[early:]:
        compress(members)
        send(members)

    names["schur"].wait()
    high, low = halves(schur[0])
    s_high[...] = high
    s_low[...] = low
    mid = slice(face, 2 * face)
    b_both, b_high = pair(in_face[1])
    force = product(s_high[:, mid], s_low[:, mid], b_both, b_high)
    @pl.when(has_above)
    def _():
        faces[0].wait_recv()

    @pl.when(has_below)
    def _():
        faces[2].wait_recv()

    for o in (0, 2):
        span = slice(o * face, (o + 1) * face)
        b_both, b_high = pair(in_face[o])
        force = force + product(s_high[:, span], s_low[:, span], b_both, b_high)
    out_force[0] = force[:face]
    out_force[1] = force[2 * face :]
    in_force[1] = force[mid]

    @pl.when(has_above)
    def _():
        returns[0].start()

    @pl.when(has_below)
    def _():
        returns[2].start()

    names["u"].wait()
    names["near"].wait()
    for at, members in enumerate(groups):
        block = jnp.concatenate([u[from_of(k)] for k in members], axis=0).T
        high, low = halves(block)
        span = slice(at * group * rank_top, (at + 1) * group * rank_top)
        u_high[:, span] = high
        u_low[:, span] = low
    near_high, near_low = halves(near[...])
    out_ref[...] = product(near_high, near_low, it_both, it_high)

    def far(first, size):
        for k, slot in slot_of.items():
            if k > 0 and first <= slot < first + size:
                copies[k].wait_recv()
        got = gathered[first : first + size].reshape(size * rank_top, loads)
        b_both, b_high = pair(got)
        span = slice(first * rank_top, (first + size) * rank_top)
        return product(u_high[:, span], u_low[:, span], b_both, b_high)

    spans = [(at * group, group) for at in range(len(groups))]
    half = len(spans) // 2
    spans = spans[half:][::-1] + spans[:half]
    if JOIN and half > 1:
        spans = spans[:-half] + [(at * group, 2 * group) for at in range(0, half - 1, 2)]
        if half % 2:
            spans = spans[:-1] + [((half - 1) * group, group), spans[-1]]
    for first, size in spans[: len(spans) - TAIL]:
        out_ref[...] += far(first, size)

    @pl.when(has_below)
    def _():
        returns[0].wait_recv()

    @pl.when(has_above)
    def _():
        returns[2].wait_recv()

    total = out_ref[...]
    place = lax.broadcasted_iota(jnp.int32, (rows_here, face), 0)
    for o in range(3):
        scatter = (place == row_of[o]).astype(F32).astype(BF16)
        b_both, _ = pair(in_force[o])
        total = total + fold(mm(scatter, b_both))
    for first, size in spans[len(spans) - TAIL :]:
        total = total + far(first, size)
    out_ref[...] = total

    @pl.when(has_below)
    def _():
        faces[0].wait_send()
        returns[2].wait_send()

    @pl.when(has_above)
    def _():
        faces[2].wait_send()
        returns[0].wait_send()

    for k in range(1, n):
        copies[k].wait_send()


def body(
    iterate, rhs, schur, near_block, u_basis, v_basis, tile_rank, send_rows, send_count, precond
):
    n = lax.axis_size("wide")
    rows_here, loads = iterate.shape
    face = send_rows.shape[2]
    tiles, rank_top, _ = u_basis.shape
    tile_rank = tile_rank.reshape(1, tiles)
    send_rows = send_rows.reshape(3, 1, face)
    dma = pltpu.SemaphoreType.DMA
    applied = pl.pallas_call(
        functools.partial(kernel, n),
        out_shape=pltpu.VMEM((rows_here, loads), F32),
        in_specs=[pl.BlockSpec(memory_space=pl.ANY)] * 8,
        out_specs=pl.BlockSpec(memory_space=pltpu.VMEM),
        scratch_shapes=[
            pltpu.VMEM(iterate.shape, F32),
            pltpu.VMEM(schur.shape, F32),
            pltpu.VMEM(near_block.shape, F32),
            pltpu.VMEM(u_basis.shape, F32),
            pltpu.VMEM(v_basis.shape, F32),
            pltpu.SMEM(tile_rank.shape, jnp.int32),
            pltpu.VMEM(send_rows.shape, jnp.int32),
            pltpu.SMEM(send_count.shape, jnp.int32),
            pltpu.VMEM((2, face, loads), F32),
            pltpu.VMEM((3, face, loads), F32),
            pltpu.VMEM((2, face, loads), F32),
            pltpu.VMEM((3, face, loads), F32),
            pltpu.VMEM((n, rank_top, loads), F32),
            pltpu.VMEM((n, rank_top, loads), F32),
            pltpu.VMEM((rows_here, tiles * rank_top), BF16),
            pltpu.VMEM((rows_here, tiles * rank_top), BF16),
            pltpu.VMEM(schur.shape[1:], BF16),
            pltpu.VMEM(schur.shape[1:], BF16),
            dma((7 + n,)),
            dma((2,)),
            dma((2,)),
            dma((2,)),
            dma((2,)),
            dma((n,)),
            dma((n,)),
        ],
        compiler_params=pltpu.CompilerParams(collective_id=0, has_side_effects=True),
    )(iterate, schur, near_block, u_basis, v_basis, tile_rank, send_rows, send_count)
    residual = rhs - applied
    updated = iterate + precond[:, None] * residual
    return (updated, residual)


def solution(mesh):
    in_specs = (
        P(("groups", "wide"), None),
        P(("groups", "wide"), None),
        P(("groups", "wide"), None, None),
        P(("groups", "wide"), None),
        P("groups", None, "wide"),
        P("groups", None, "wide"),
        P("groups", "wide"),
        P(("groups", "wide"), None, None),
        P(("groups", "wide"), None),
        P(("groups", "wide")),
    )
    out_specs = (P(("groups", "wide"), None), P(("groups", "wide"), None))
    return jax.shard_map(body, mesh=mesh, in_specs=in_specs, out_specs=out_specs, check_vma=False)
```
